512 devices in a mesh: vox: 16 (over x_hi, y, core), filt: 32 (over x_lo, z).
Axes of the slice: x: 4 (x_hi: 2, x_lo: 2; x = x_hi * 2 + x_lo), y: 4, z: 16, core: 2. Of those that a mesh axis runs over, the one named last changes fastest.
Arguments:
- volume: bfloat16 [1024, 64, 128], P('filt', 'vox'), may hold values from -6 to 6
- kernel: bfloat16 [27, 1024, 1024], P(None, 'filt', 'vox'), may hold values from -0.0390625 to 0.0390625
- bias: float32 [1024], P('filt'), may hold values from -3 to 3
Outputs:
- features: bfloat16 [1024, 64, 128], P('filt', 'vox')
The draws below stay inside these ranges and needn't reach their ends.
All inputs are finite; a program needn't handle non-finite values.
Results may differ from the reference program's by a relative error of at most 0.001.
Values may be sent and summed in bfloat16 or wider, within the bound.
No kernel may reach another device: no remote copies, remote signals or barrier semaphores. Data moves between devices by JAX's collectives and lax.ppermute only.
A program may use at most 64 MiB of HBM per device.

```python
import jax
import jax.numpy as jnp
from jax import lax

C_IN = 1024
C_OUT = 1024
H = 4
W = 32
DEPTH = 64


def level_of(key, shape, pieces, least, high):
    gain, own = 1.0, jax.random.fold_in(key, 6)
    for position, blocks in pieces:
        heights = jnp.exp(jax.random.uniform(jax.random.fold_in(own, position), (blocks,), jnp.float32, least / len(pieces), high / len(pieces)))
        gain = gain * jnp.repeat(heights, shape[position] // blocks).reshape([-1 if axis == position else 1 for axis in range(len(shape))])
    return gain


def centred(key, shape, scale, limit, pieces=(), dtype=jnp.bfloat16):
    values = jax.random.normal(key, shape, jnp.float32) * scale
    if len(pieces) > 0:
        values = level_of(key, shape, pieces, -0.22, 0.18) * values
    return jnp.clip(values, min=-limit, max=limit).astype(dtype)


def setup_inputs(seed: int = 0) -> dict:
    key_list = jax.random.split(jax.random.key(seed), 4)
    volume = centred(key_list[0], (C_IN, DEPTH, H * W), 1.0, 6.0, ((0, 32), (1, 16)))
    kernel = centred(key_list[1], (27, C_OUT, C_IN), (27 * C_IN) ** -0.5, 0.0390625, ((1, 32), (2, 16)))
    bias = centred(key_list[2], (C_OUT,), 0.5, 3.0, ((0, 32),), jnp.float32)
    return dict(volume=volume, kernel=kernel, bias=bias)


def reference(volume, kernel, bias):
    channels = volume.shape[0]
    depth_all = volume.shape[1]
    filters = kernel.shape[1]
    volume_wide = volume.astype(jnp.float32).reshape(1, channels, depth_all, H, W)
    kernel_wide = kernel.astype(jnp.float32).reshape(3, 3, 3, filters, channels)
    summed = lax.conv_general_dilated(volume_wide, kernel_wide, (1, 1, 1), [(1, 1), (1, 1), (1, 1)], dimension_numbers=("NCDHW", "DHWOI", "NCDHW"), precision=lax.Precision.HIGHEST)
    result = summed[0] + bias[:, None, None, None]
    return result.reshape(filters, depth_all, H * W).astype(jnp.bfloat16)
```

```python
import jax
import jax.numpy as jnp
from jax import lax
from jax.experimental import pallas as pl
from jax.experimental.pallas import tpu as pltpu
from jax.sharding import Mesh, PartitionSpec as P


AXES = ("xh", "y", "core", "xl", "z")
LANES = 128
TAPS = 27
FILT = 32
ROWS = TAPS * FILT
HALF = ROWS // 2


def pack_kernel(w_ref, o_ref):
    w = w_ref[...].reshape(ROWS, 64)
    o_ref[...] = jnp.concatenate([w[:HALF], w[HALF:]], axis=1)


def pack(kernel):
    return pl.pallas_call(
        pack_kernel,
        out_shape=jax.ShapeDtypeStruct((HALF, LANES), jnp.bfloat16),
        in_specs=[pl.BlockSpec(memory_space=pltpu.VMEM)],
        out_specs=pl.BlockSpec(memory_space=pltpu.VMEM),
        name="pack",
    )(kernel)


def conv_kernel(s_ref, own_ref, pair_ref, x_ref, lo_ref, hi_ref, o_ref, xs, zs):
    swap = s_ref[0]
    y = s_ref[1]
    core = s_ref[2]
    for dy in range(4):
        q = lax.rem(y + dy, 4)
        for part in range(2):
            rows = slice(dy * 128 + part * 64, dy * 128 + part * 64 + 64)
            z = pl.ds(4 * q + 2 * (core ^ part), 2)
            xs[rows, 0:128] = lo_ref[z].reshape(64, LANES)
            xs[rows, 640:768] = hi_ref[z].reshape(64, LANES)
            for d in range(4):
                xs[rows, (d + 1) * 128 : (d + 2) * 128] = x_ref[z, d].reshape(64, LANES)
    lane = lax.broadcasted_iota(jnp.int32, (FILT, LANES), 1)
    row, cell = lane // 32, lane % 32
    for r in range(2):
        first = []
        second = []
        for dy in range(4):
            a = own_ref[4 * r + dy]
            b = pair_ref[4 * r + dy]
            first.append(jnp.concatenate([a[:, :64], b[:, :64]], axis=1))
            second.append(jnp.concatenate([a[:, 64:], b[:, 64:]], axis=1))
        zs[0:HALF] = jnp.dot(jnp.concatenate(first, axis=1), xs[...], preferred_element_type=jnp.float32)
        zs[HALF:ROWS] = jnp.dot(jnp.concatenate(second, axis=1), xs[...], preferred_element_type=jnp.float32)
        for d in range(4):
            total = None
            for b in range(3):
                for e in range(3):
                    part = None
                    for a in range(3):
                        tap = 9 * a + 3 * b + e
                        piece = zs[tap * FILT : (tap + 1) * FILT, (d + a) * 128 : (d + a + 1) * 128]
                        part = piece if part is None else part + piece
                    shift = (b - 1) * 32 + (e - 1)
                    if shift != 0:
                        part = pltpu.roll(part, (-shift) % LANES, 1)
                        ok = (row + (b - 1) >= 0) & (row + (b - 1) < 4) & (cell + (e - 1) >= 0) & (cell + (e - 1) < 32)
                        part = jnp.where(ok, part, 0.0)
                    total = part if total is None else total + part
            o_ref[r ^ swap, d] = total


def conv(scalars, own, pair, x, lo, hi):
    vm = pl.BlockSpec(memory_space=pltpu.VMEM)
    return pl.pallas_call(
        conv_kernel,
        out_shape=jax.ShapeDtypeStruct((2, 4, FILT, LANES), jnp.float32),
        in_specs=[pl.BlockSpec(memory_space=pltpu.SMEM), vm, vm, vm, vm, vm],
        out_specs=vm,
        scratch_shapes=[pltpu.VMEM((512, 768), jnp.bfloat16), pltpu.VMEM((ROWS, 768), jnp.float32)],
        name="conv",
    )(scalars, own, pair, x, lo, hi)


def flat(xh, y, xl):
    return (xh * 4 + y) * 2 + xl


def work(volume, kernel, bias):
    xh = lax.axis_index("xh")
    xl = lax.axis_index("xl")
    y = lax.axis_index("y")
    x = volume.transpose(1, 0, 2)
    spread = jnp.broadcast_to(x[None], (16,) + x.shape)
    x_all = lax.all_to_all(spread, "z", 0, 0, tiled=True)
    packed = pack(kernel)
    pieces = []
    for r in range(2):
        for dy in range(4):
            pairs = [
                (flat(tl, (ty + dy) % 4, (th + r) % 2), flat(th, ty, tl))
                for th in range(2)
                for ty in range(4)
                for tl in range(2)
            ]
            pieces.append(lax.ppermute(packed, ("xh", "y", "xl"), pairs))
    own = jnp.stack(pieces)
    pair = lax.ppermute(own, "core", [(0, 1), (1, 0)])
    up = [(i, i + 1) for i in range(15)]
    down = [(i + 1, i) for i in range(15)]
    lo = lax.ppermute(x_all[:, 3], ("xh", "y", "core"), up)
    hi = lax.ppermute(x_all[:, 0], ("xh", "y", "core"), down)
    scalars = jnp.stack([jnp.bitwise_xor(xh, xl), y, lax.axis_index("core")]).astype(jnp.int32)
    partial = conv(scalars, own, pair, x_all, lo, hi)
    other = lax.ppermute(partial[1], "xl", [(0, 1), (1, 0)])
    out = partial[0] + other + bias[None, :, None]
    return out.astype(jnp.bfloat16).transpose(1, 0, 2)


def solution(mesh):
    fine = Mesh(mesh.devices.reshape(2, 4, 2, 2, 16), AXES)
    vox = ("xh", "y", "core")
    filt = ("xl", "z")
    in_specs = (P(filt, vox, None), P(None, filt, vox), P(filt))
    return jax.shard_map(work, mesh=fine, in_specs=in_specs, out_specs=P(filt, vox, None), check_vma=False)
```

```python
import jax
import jax.numpy as jnp
from jax import lax
from jax.experimental import pallas as pl
from jax.experimental.pallas import tpu as pltpu
from jax.sharding import Mesh, PartitionSpec as P


AXES = ("xh", "y", "core", "xl", "z")
LANES = 128
TAPS = 27
FILT = 32
ROWS = TAPS * FILT
HALF = ROWS // 2
VM = pl.BlockSpec(memory_space=pltpu.VMEM)


def spread_kernel(x_ref, o_ref):
    for d in range(4):
        plane = x_ref[:, d, :]
        for z in range(16):
            o_ref[z, d] = plane


def spread(volume):
    return pl.pallas_call(
        spread_kernel,
        out_shape=jax.ShapeDtypeStruct((16, 4, FILT, LANES), jnp.bfloat16),
        in_specs=[VM],
        out_specs=VM,
        name="spread",
    )(volume)


def pack_kernel(w_ref, o_ref):
    w = w_ref[...].reshape(ROWS, 64)
    o_ref[...] = jnp.concatenate([w[:HALF], w[HALF:]], axis=1)


def pack(kernel):
    return pl.pallas_call(
        pack_kernel,
        out_shape=jax.ShapeDtypeStruct((HALF, LANES), jnp.bfloat16),
        in_specs=[VM],
        out_specs=VM,
        name="pack",
    )(kernel)


def conv_kernel(flip, own_ref, pair_ref, x_ref, near_ref, far_ref, o_ref, xs, zs):
    core = lax.axis_index("core")
    group = lax.axis_index("xl") ^ lax.axis_index("xh") ^ flip
    for dy in range(4):
        q = dy
        for part in range(2):
            rows = slice(dy * 128 + part * 64, dy * 128 + part * 64 + 64)
            z = pl.ds(4 * q + 2 * (core ^ part), 2)
            xs[rows, pl.ds(pl.multiple_of(640 * (1 - core), 128), 128)] = near_ref[z].reshape(64, LANES)
            xs[rows, pl.ds(pl.multiple_of(640 * core, 128), 128)] = far_ref[z].reshape(64, LANES)
            for d in range(4):
                xs[rows, (d + 1) * 128 : (d + 2) * 128] = x_ref[z, d].reshape(64, LANES)
    lane = lax.broadcasted_iota(jnp.int32, (FILT, LANES), 1)
    row, cell = lane // 32, lane % 32
    first = []
    second = []
    for dy in range(4):
        a = own_ref[dy, group]
        b = pair_ref[dy, group]
        first.append(jnp.concatenate([a[:, :64], b[:, :64]], axis=1))
        second.append(jnp.concatenate([a[:, 64:], b[:, 64:]], axis=1))
    zs[0:HALF] = jnp.dot(jnp.concatenate(first, axis=1), xs[...], preferred_element_type=jnp.float32)
    zs[HALF:ROWS] = jnp.dot(jnp.concatenate(second, axis=1), xs[...], preferred_element_type=jnp.float32)
    for d in range(4):
        total = None
        for b in range(3):
            for e in range(3):
                part = None
                for a in range(3):
                    tap = 9 * a + 3 * b + e
                    piece = zs[tap * FILT : (tap + 1) * FILT, (d + a) * 128 : (d + a + 1) * 128]
                    part = piece if part is None else part + piece
                shift = (b - 1) * 32 + (e - 1)
                if shift != 0:
                    part = pltpu.roll(part, (-shift) % LANES, 1)
                    ok = (row + (b - 1) >= 0) & (row + (b - 1) < 4) & (cell + (e - 1) >= 0) & (cell + (e - 1) < 32)
                    part = jnp.where(ok, part, 0.0)
                total = part if total is None else total + part
        o_ref[d] = total


def conv(flip, own, pair, x, near, far):
    def body(*refs):
        conv_kernel(flip, *refs)

    return pl.pallas_call(
        body,
        out_shape=jax.ShapeDtypeStruct((4, FILT, LANES), jnp.float32),
        in_specs=[VM] * 5,
        out_specs=VM,
        scratch_shapes=[pltpu.VMEM((512, 768), jnp.bfloat16), pltpu.VMEM((ROWS, 768), jnp.float32)],
        name="conv_send" if flip else "conv_keep",
    )(own, pair, x, near, far)


def work(volume, kernel, bias):
    spread_x = spread(volume)
    x_all = lax.all_to_all(spread_x, "z", 0, 0, tiled=True)
    packed = pack(kernel)
    turned = []
    for r in range(2):
        pairs = [(2 * tl + (th + r) % 2, 2 * th + tl) for th in range(2) for tl in range(2)]
        turned.append(lax.ppermute(packed, ("xh", "xl"), pairs))
    both = jnp.stack(turned)
    own = lax.all_gather(both, "y", axis=0, tiled=False)
    pair = lax.ppermute(own, "core", [(0, 1), (1, 0)])
    core = lax.axis_index("core")
    outside = [(i, i - 1) if i % 2 == 0 else (i, i + 1) for i in range(1, 15)]
    near = lax.dynamic_index_in_dim(x_all, 3 * (1 - core), 1, keepdims=False)
    far = lax.dynamic_index_in_dim(x_all, 3 * core, 1, keepdims=False)
    far = lax.ppermute(far, ("xh", "y", "core"), outside)
    near = lax.ppermute(near, "core", [(0, 1), (1, 0)])
    own, pair, x_all, near, far = (pltpu.with_memory_space_constraint(v, pltpu.VMEM) for v in (own, pair, x_all, near, far))
    send = conv(1, own, pair, x_all, near, far)
    other = lax.ppermute(send, "xl", [(0, 1), (1, 0)])
    keep = conv(0, own, pair, x_all, near, far)
    return (keep + other + bias[None, :, None]).astype(jnp.bfloat16).transpose(1, 0, 2)


def solution(mesh):
    fine = Mesh(mesh.devices.reshape(2, 4, 2, 2, 16), AXES)
    vox = ("xh", "y", "core")
    filt = ("xl", "z")
    in_specs = (P(filt, vox, None), P(None, filt, vox), P(filt))
    return jax.shard_map(work, mesh=fine, in_specs=in_specs, out_specs=P(filt, vox, None), check_vma=False)
```

```python
import jax
import jax.numpy as jnp
from jax import lax
from jax.experimental import pallas as pl
from jax.experimental.pallas import tpu as pltpu
from jax.sharding import Mesh, PartitionSpec as P


AXES = ("xh", "y", "core", "xl", "z")
LANES = 128
TAPS = 27
FILT = 32
ROWS = TAPS * FILT
HALF = ROWS // 2
VM = pl.BlockSpec(memory_space=pltpu.VMEM)


def order_rows(x, outer):
    inner = 128 // outer
    i = lax.broadcasted_iota(jnp.int32, (128, 128), 0)
    j = lax.broadcasted_iota(jnp.int32, (128, 128), 1)
    pick = (j == lax.rem(i, inner) * outer + lax.div(i, inner)).astype(jnp.bfloat16)
    return jnp.dot(pick, x, preferred_element_type=jnp.float32).astype(jnp.bfloat16)


def spread_kernel(x_ref, o_ref):
    planes = order_rows(x_ref[...], 4).reshape(4, FILT, LANES)
    for z in range(16):
        o_ref[z] = planes


def spread(volume):
    return pl.pallas_call(
        spread_kernel,
        out_shape=jax.ShapeDtypeStruct((16, 4, FILT, LANES), jnp.bfloat16),
        in_specs=[VM],
        out_specs=VM,
        name="spread",
    )(volume.reshape(4 * FILT, LANES))


def finish_kernel(keep_ref, other_ref, column_ref, o_ref):
    total = (keep_ref[...] + other_ref[1 - lax.axis_index("xl")] + column_ref[...]).astype(jnp.bfloat16)
    o_ref[...] = order_rows(total.reshape(4 * FILT, LANES), FILT)


def finish(keep, other, column):
    return pl.pallas_call(
        finish_kernel,
        out_shape=jax.ShapeDtypeStruct((4 * FILT, LANES), jnp.bfloat16),
        in_specs=[VM] * 3,
        out_specs=VM,
        name="finish",
    )(keep, other, column).reshape(FILT, 4, LANES)


def pack_kernel(w_ref, bias_ref, o_ref, column_ref):
    w = w_ref[...].reshape(ROWS, 64)
    o_ref[...] = jnp.concatenate([w[:HALF], w[HALF:]], axis=1)
    i = lax.broadcasted_iota(jnp.int32, (FILT, FILT), 0)
    j = lax.broadcasted_iota(jnp.int32, (FILT, FILT), 1)
    column = jnp.sum(jnp.where(i == j, bias_ref[...], 0.0), axis=1, keepdims=True)
    column_ref[...] = jnp.broadcast_to(column, (FILT, LANES))


def pack(kernel, bias):
    return pl.pallas_call(
        pack_kernel,
        out_shape=[jax.ShapeDtypeStruct((HALF, LANES), jnp.bfloat16), pltpu.VMEM((FILT, LANES), jnp.float32)],
        in_specs=[VM] * 2,
        out_specs=[VM] * 2,
        name="pack",
    )(kernel, bias)


def conv_kernel(own_ref, pair_ref, x_ref, near_ref, far_ref, send_ref, keep_ref, xs, zs):
    core = lax.axis_index("core")
    slot = lax.axis_index("xl") ^ lax.axis_index("xh")
    for dy in range(4):
        q = dy
        for part in range(2):
            rows = slice(dy * 128 + part * 64, dy * 128 + part * 64 + 64)
            z = pl.ds(4 * q + 2 * (core ^ part), 2)
            xs[rows, pl.ds(pl.multiple_of(640 * (1 - core), 128), 128)] = near_ref[z].reshape(64, LANES)
            xs[rows, pl.ds(pl.multiple_of(640 * core, 128), 128)] = far_ref[z].reshape(64, LANES)
            for d in range(4):
                xs[rows, (d + 1) * 128 : (d + 2) * 128] = x_ref[z, d].reshape(64, LANES)
    lane = lax.broadcasted_iota(jnp.int32, (FILT, LANES), 1)
    row, cell = lane // 32, lane % 32
    for flip, o_ref in ((1, send_ref), (0, keep_ref)):
        group = slot ^ flip
        first = []
        second = []
        for dy in range(4):
            a = own_ref[dy, group]
            b = pair_ref[dy, group]
            first.append(jnp.concatenate([a[:, :64], b[:, :64]], axis=1))
            second.append(jnp.concatenate([a[:, 64:], b[:, 64:]], axis=1))
        first = jnp.concatenate(first, axis=1)
        second = jnp.concatenate(second, axis=1)
        for part in range(2):
            lead = 144 * part
            blocks = (
                first[lead : lead + 144],
                (second[0:144] if part else first[288:432]),
                second[lead + 144 : lead + 288],
            )
            zs[lead : lead + 144] = sum(
                jnp.dot(w, xs[:, 128 * a : 128 * a + 512], preferred_element_type=jnp.float32) for a, w in enumerate(blocks)
            )
        for d in range(4):
            total = None
            for b in range(3):
                for e in range(3):
                    at = (3 * b + e) * FILT
                    part = zs[at : at + FILT, d * 128 : (d + 1) * 128]
                    shift = (b - 1) * 32 + (e - 1)
                    if shift != 0:
                        part = pltpu.roll(part, (-shift) % LANES, 1)
                        ok = (row + (b - 1) >= 0) & (row + (b - 1) < 4) & (cell + (e - 1) >= 0) & (cell + (e - 1) < 32)
                        part = jnp.where(ok, part, 0.0)
                    total = part if total is None else total + part
            o_ref[d] = total


def conv(own, pair, x, near, far):
    return pl.pallas_call(
        conv_kernel,
        out_shape=[pltpu.VMEM((4, FILT, LANES), jnp.float32)] * 2,
        in_specs=[VM] * 5,
        out_specs=[VM] * 2,
        scratch_shapes=[pltpu.VMEM((512, 768), jnp.bfloat16), pltpu.VMEM((ROWS // 3, 512), jnp.float32)],
        name="conv",
    )(own, pair, x, near, far)


def work(volume, kernel, bias):
    spread_x = spread(volume)
    x_all = lax.all_to_all(spread_x, "z", 0, 0, tiled=True)
    kernel, bias = (pltpu.with_memory_space_constraint(v, pltpu.VMEM) for v in (kernel, bias.reshape(1, FILT)))
    packed, column = pack(kernel, bias)
    turned = []
    for r in range(2):
        pairs = [(2 * tl + (th + r) % 2, 2 * th + tl) for th in range(2) for tl in range(2)]
        turned.append(lax.ppermute(packed, ("xh", "xl"), pairs))
    both = jnp.stack(turned)
    own = lax.all_gather(both, "y", axis=0, tiled=False)
    pair = lax.ppermute(own, "core", [(0, 1), (1, 0)])
    core = lax.axis_index("core")
    outside = [(i, i - 1) if i % 2 == 0 else (i, i + 1) for i in range(1, 15)]
    near = lax.dynamic_index_in_dim(x_all, 3 * (1 - core), 1, keepdims=False)
    far = lax.dynamic_index_in_dim(x_all, 3 * core, 1, keepdims=False)
    near = lax.ppermute(near, "core", [(0, 1), (1, 0)])
    far = lax.ppermute(far, ("xh", "y", "core"), outside)
    own, pair, x_all, near, far = (pltpu.with_memory_space_constraint(v, pltpu.VMEM) for v in (own, pair, x_all, near, far))
    send, keep = conv(own, pair, x_all, near, far)
    other = lax.all_gather(send, "xl", axis=0, tiled=False)
    keep, other = (pltpu.with_memory_space_constraint(v, pltpu.VMEM) for v in (keep, other))
    return finish(keep, other, pltpu.with_memory_space_constraint(column, pltpu.VMEM))


def solution(mesh):
    fine = Mesh(mesh.devices.reshape(2, 4, 2, 2, 16), AXES)
    vox = ("xh", "y", "core")
    filt = ("xl", "z")
    in_specs = (P(filt, vox, None), P(None, filt, vox), P(filt))
    return jax.shard_map(work, mesh=fine, in_specs=in_specs, out_specs=P(filt, vox, None), check_vma=False)
```

```python
import jax
import jax.numpy as jnp
from jax import lax
from jax.experimental import pallas as pl
from jax.experimental.pallas import tpu as pltpu
from jax.sharding import Mesh, PartitionSpec as P


AXES = ("xh", "y", "core", "xl", "z")
LANES = 128
TAPS = 27
FILT = 32
ROWS = TAPS * FILT
HALF = ROWS // 2
VM = pl.BlockSpec(memory_space=pltpu.VMEM)


def order_rows(x, outer):
    inner = 128 // outer
    i = lax.broadcasted_iota(jnp.int32, (128, 128), 0)
    j = lax.broadcasted_iota(jnp.int32, (128, 128), 1)
    pick = (j == lax.rem(i, inner) * outer + lax.div(i, inner)).astype(jnp.bfloat16)
    return jnp.dot(pick, x, preferred_element_type=jnp.float32).astype(jnp.bfloat16)


def spread_kernel(x_ref, o_ref):
    planes = order_rows(x_ref[...], 4).reshape(4, FILT, LANES)
    for z in range(16):
        o_ref[z] = planes


def spread(volume):
    return pl.pallas_call(
        spread_kernel,
        out_shape=pltpu.VMEM((16, 4, FILT, LANES), jnp.bfloat16),
        in_specs=[VM],
        out_specs=VM,
        name="spread",
    )(pltpu.with_memory_space_constraint(volume.reshape(4 * FILT, LANES), pltpu.VMEM))


def finish_kernel(keep_ref, other_ref, column_ref, o_ref):
    total = (keep_ref[...] + other_ref[1 - lax.axis_index("xl")] + column_ref[...]).astype(jnp.bfloat16)
    o_ref[...] = order_rows(total.reshape(4 * FILT, LANES), FILT)


def finish(keep, other, column):
    return pl.pallas_call(
        finish_kernel,
        out_shape=jax.ShapeDtypeStruct((4 * FILT, LANES), jnp.bfloat16),
        in_specs=[VM] * 3,
        out_specs=VM,
        name="finish",
    )(keep, other, column).reshape(FILT, 4, LANES)


def pack_kernel(w_ref, bias_ref, o_ref, column_ref):
    w = w_ref[...].reshape(ROWS, 64)
    o_ref[...] = jnp.concatenate([w[:HALF], w[HALF:]], axis=1)
    i = lax.broadcasted_iota(jnp.int32, (FILT, FILT), 0)
    j = lax.broadcasted_iota(jnp.int32, (FILT, FILT), 1)
    column = jnp.sum(jnp.where(i == j, bias_ref[...], 0.0), axis=1, keepdims=True)
    column_ref[...] = jnp.broadcast_to(column, (FILT, LANES))


def pack(kernel, bias):
    return pl.pallas_call(
        pack_kernel,
        out_shape=[jax.ShapeDtypeStruct((HALF, LANES), jnp.bfloat16), pltpu.VMEM((FILT, LANES), jnp.float32)],
        in_specs=[VM] * 2,
        out_specs=[VM] * 2,
        name="pack",
    )(kernel, bias)


def conv_kernel(own_ref, pair_ref, x_ref, near_ref, far_ref, send_ref, keep_ref, xs, zs):
    core = lax.axis_index("core")
    slot = lax.axis_index("xl") ^ lax.axis_index("xh")
    for dy in range(4):
        q = dy
        for part in range(2):
            rows = slice(dy * 128 + part * 64, dy * 128 + part * 64 + 64)
            z = pl.ds(4 * q + 2 * (core ^ part), 2)
            xs[rows, pl.ds(pl.multiple_of(640 * (1 - core), 128), 128)] = near_ref[1 - core, z].reshape(64, LANES)
            xs[rows, pl.ds(pl.multiple_of(640 * core, 128), 128)] = far_ref[z].reshape(64, LANES)
            for d in range(4):
                xs[rows, (d + 1) * 128 : (d + 2) * 128] = x_ref[z, d].reshape(64, LANES)
    lane = lax.broadcasted_iota(jnp.int32, (FILT, LANES), 1)
    row, cell = lane // 32, lane % 32
    for flip, o_ref in ((1, send_ref), (0, keep_ref)):
        group = slot ^ flip
        first = []
        second = []
        for dy in range(4):
            a = own_ref[dy, group]
            b = pair_ref[dy, group]
            first.append(jnp.concatenate([a[:, :64], b[:, :64]], axis=1))
            second.append(jnp.concatenate([a[:, 64:], b[:, 64:]], axis=1))
        first = jnp.concatenate(first, axis=1)
        second = jnp.concatenate(second, axis=1)
        for part in range(2):
            lead = 144 * part
            blocks = (
                first[lead : lead + 144],
                (second[0:144] if part else first[288:432]),
                second[lead + 144 : lead + 288],
            )
            zs[lead : lead + 144] = sum(
                jnp.dot(w, xs[:, 128 * a : 128 * a + 512], preferred_element_type=jnp.float32) for a, w in enumerate(blocks)
            )
        for d in range(4):
            total = None
            for b in range(3):
                for e in range(3):
                    at = (3 * b + e) * FILT
                    part = zs[at : at + FILT, d * 128 : (d + 1) * 128]
                    shift = (b - 1) * 32 + (e - 1)
                    if shift != 0:
                        part = pltpu.roll(part, (-shift) % LANES, 1)
                        ok = (row + (b - 1) >= 0) & (row + (b - 1) < 4) & (cell + (e - 1) >= 0) & (cell + (e - 1) < 32)
                        part = jnp.where(ok, part, 0.0)
                    total = part if total is None else total + part
            o_ref[d] = total


def conv(own, pair, x, near, far):
    return pl.pallas_call(
        conv_kernel,
        out_shape=[pltpu.VMEM((4, FILT, LANES), jnp.float32)] * 2,
        in_specs=[VM] * 5,
        out_specs=[VM] * 2,
        scratch_shapes=[pltpu.VMEM((512, 768), jnp.bfloat16), pltpu.VMEM((ROWS // 3, 512), jnp.float32)],
        name="conv",
    )(own, pair, x, near, far)


def work(volume, kernel, bias):
    spread_x = spread(volume)
    x_all = lax.all_to_all(spread_x, "z", 0, 0, tiled=True)
    kernel, bias = (pltpu.with_memory_space_constraint(v, pltpu.VMEM) for v in (kernel, bias.reshape(1, FILT)))
    packed, column = pack(kernel, bias)
    turned = []
    for r in range(2):
        pairs = [(2 * tl + (th + r) % 2, 2 * th + tl) for th in range(2) for tl in range(2)]
        turned.append(lax.ppermute(packed, ("xh", "xl"), pairs))
    both = jnp.stack(turned)
    own = lax.all_gather(both, "y", axis=0, tiled=False)
    pair = lax.ppermute(own, "core", [(0, 1), (1, 0)])
    core = lax.axis_index("core")
    outside = [(i, i - 1) if i % 2 == 0 else (i, i + 1) for i in range(1, 15)]
    near = lax.dynamic_index_in_dim(x_all, 3 * (1 - core), 1, keepdims=False)
    far = lax.dynamic_index_in_dim(x_all, 3 * core, 1, keepdims=False)
    near = lax.all_gather(near, "core", axis=0, tiled=False)
    far = lax.ppermute(far, ("xh", "y", "core"), outside)
    own, pair, x_all, near, far = (pltpu.with_memory_space_constraint(v, pltpu.VMEM) for v in (own, pair, x_all, near, far))
    send, keep = conv(own, pair, x_all, near, far)
    other = lax.all_gather(send, "xl", axis=0, tiled=False)
    keep, other = (pltpu.with_memory_space_constraint(v, pltpu.VMEM) for v in (keep, other))
    return finish(keep, other, pltpu.with_memory_space_constraint(column, pltpu.VMEM))


def solution(mesh):
    fine = Mesh(mesh.devices.reshape(2, 4, 2, 2, 16), AXES)
    vox = ("xh", "y", "core")
    filt = ("xl", "z")
    in_specs = (P(filt, vox, None), P(None, filt, vox), P(filt))
    return jax.shard_map(work, mesh=fine, in_specs=in_specs, out_specs=P(filt, vox, None), check_vma=False)
```
